256 devices in a mesh: grp: 2 (over core), mr: 16 (over y_lo, z), mc: 8 (over y_hi, x).
Axes of the slice: x: 4, y: 4 (y_hi: 2, y_lo: 2; y = y_hi * 2 + y_lo), z: 8, core: 2. Of those that a mesh axis runs over, the one named last changes fastest.
Arguments:
- queries: bfloat16 [768, 8192], P(('grp', 'mr'), 'mc'), may hold values from -6 to 6
- new_keys: bfloat16 [768, 1024], P(('grp', 'mr'), 'mc'), may hold values from -6 to 6
- new_values: bfloat16 [768, 1024], P(('grp', 'mr'), 'mc'), may hold values from -6 to 6
- key_cache: bfloat16 [768, 512, 1024], P(('grp', 'mr'), None, 'mc'), may hold values from -6 to 6
- value_cache: bfloat16 [768, 512, 1024], P(('grp', 'mr'), None, 'mc'), may hold values from -6 to 6
- context_len: int32 [768], P(('grp', 'mr')), may hold values from 2 to 512, as said below
- cache_slot: int32 [768], P(('grp', 'mr')), may hold values from 0 to 767, as said below
- residual_in: bfloat16 [768, 8192], P(('grp', 'mr'), 'mc'), may hold values from -31 to 31
- out_weight: bfloat16 [8192, 8192], P(('grp', 'mr'), 'mc'), may hold values from -0.25 to 0.25
- gate_weight: bfloat16 [8192, 28672], P('mc', ('grp', 'mr')), may hold values from -0.0625 to 0.0625
- up_weight: bfloat16 [8192, 28672], P('mc', ('grp', 'mr')), may hold values from -0.0625 to 0.0625
Outputs:
- residual_out: bfloat16 [768, 8192], P(('grp', 'mr'), 'mc')
- activation: bfloat16 [768, 28672], P('mc', ('grp', 'mr'))
The draws below stay inside these ranges and needn't reach their ends.
Inputs may be any that keep to these rules, and one draw needn't show every extreme that they name: Row r's history fills positions 0 to context_len[r] - 1 of its cache row; some row has 512. `cache_slot`: within each aligned block of 24 rows the values are a permutation of that block's own row indices.
All inputs are finite; a program needn't handle non-finite values.
Results may differ from the reference program's by a relative error of at most 0.006.
Values may be sent and summed in bfloat16 or wider, within the bound.
No kernel may reach another device: no remote copies, remote signals or barrier semaphores. Data moves between devices by JAX's collectives and lax.ppermute only.
A program may use at most 64 MiB of HBM per device.

```python
import jax
import jax.numpy as jnp
from jax import lax

D = 8192
H = 64
KVH = 8
HD = 128
FF = 28672
CTX = 512
ROWS_DEV = 24
ROWS = 768


def draw_queries(key, part):
    current_key = jax.random.fold_in(key, 17)
    values = jax.random.truncated_normal(current_key, -6.0, 6.0, (ROWS, H * HD), jnp.float32)
    return values.astype(jnp.bfloat16)


def draw_key_cache(key, part):
    current_key = jax.random.fold_in(key, 29)
    values = jax.random.truncated_normal(current_key, -6.0, 6.0, (ROWS, CTX, KVH * HD), jnp.float32)
    return values.astype(jnp.bfloat16)


def draw_residual_in(key, part):
    column = jnp.arange(D, dtype=jnp.float32) / D
    values = jax.random.truncated_normal(key, -6.0, 6.0, (ROWS, D), jnp.float32) * (3.0 ** column)[None, :]
    return values.astype(jnp.bfloat16)


def draw_context_len(key, part):
    length_key, longest_key = jax.random.split(jax.random.fold_in(key, 41))
    values = jax.random.randint(length_key, (ROWS,), 2, CTX + 1)
    longest = jax.random.randint(longest_key, (), 0, ROWS)
    return jnp.where(jnp.arange(ROWS) == longest, CTX, values).astype(jnp.int32)


def shuffle_block(tile_key_rows):
    return jax.random.permutation(tile_key_rows, ROWS_DEV)


def draw_cache_slot(key, part):
    block_count = ROWS // ROWS_DEV
    block_keys = jax.random.split(jax.random.fold_in(key, 53), block_count)
    orders = jax.vmap(shuffle_block)(block_keys)
    offsets = jnp.arange(block_count, dtype=jnp.int32)[:, None] * ROWS_DEV
    return (orders.astype(jnp.int32) + offsets).reshape(ROWS).astype(jnp.int32)


def block_scale(key, dims, cuts, low, largest):
    gain = 1.0
    for dim, blocks in cuts:
        draws = jax.random.uniform(jax.random.fold_in(jax.random.fold_in(key, 6), dim), (blocks,), jnp.float32, low / len(cuts), largest / len(cuts))
        gain = gain * jnp.repeat(jnp.exp(draws), dims[dim] // blocks).reshape((-1,) + (1,) * (len(dims) - 1 - dim))
    return gain


def scatter_about(rng, shape, scale, bound, pieces=(), kind=jnp.bfloat16):
    array = jax.random.normal(rng, shape, jnp.float32) * scale
    if len(pieces) > 0:
        array = block_scale(rng, shape, pieces, -0.22, 0.18) * array
    return jnp.clip(array, min=-bound, max=bound).astype(kind)


def setup_inputs(seed: int = 0) -> dict:
    key_list = jax.random.split(jax.random.key(seed), 12)
    queries = draw_queries(jax.random.fold_in(key_list[11], 71), 0)
    new_keys = scatter_about(key_list[1], (ROWS, KVH * HD), 1.0, 6.0, ((0, 32), (1, 8)))
    new_values = scatter_about(key_list[2], (ROWS, KVH * HD), 1.0, 6.0, ((0, 32), (1, 8)))
    key_cache = draw_key_cache(jax.random.fold_in(key_list[11], 71), 0)
    value_cache = scatter_about(key_list[4], (ROWS, CTX, KVH * HD), 1.0, 6.0, ((0, 32), (2, 8)))
    context_len = draw_context_len(jax.random.fold_in(key_list[11], 71), 0)
    cache_slot = draw_cache_slot(jax.random.fold_in(key_list[11], 71), 0)
    residual_in = draw_residual_in(jax.random.fold_in(key_list[11], 71), 0)
    out_weight = scatter_about(key_list[8], (H * HD, D), (H * 8) ** -0.5, 0.25, ((0, 32), (1, 8)))
    gate_weight = scatter_about(key_list[9], (D, FF), D ** -0.5, 0.0625, ((0, 8), (1, 32)))
    up_weight = scatter_about(key_list[10], (D, FF), D ** -0.5, 0.0625, ((0, 8), (1, 32)))
    return {"queries": queries, "new_keys": new_keys, "new_values": new_values, "key_cache": key_cache, "value_cache": value_cache, "context_len": context_len, "cache_slot": cache_slot, "residual_in": residual_in, "out_weight": out_weight, "gate_weight": gate_weight, "up_weight": up_weight}


norm_epsilon = 1e-05
masked_score = -1e+30

def attend_block(queries, new_keys, new_values, key_rows, value_rows, context_len):
    row_denominator_sum = queries.shape[0]
    kv_heads = key_rows.shape[2] // HD
    groups = queries.shape[1] // key_rows.shape[2]
    attention_logit_scale = HD ** (-0.5)
    query_grouped_four = queries.astype(jnp.float32).reshape(row_denominator_sum, kv_heads, groups, HD)
    key_four = key_rows.astype(jnp.float32).reshape(row_denominator_sum, CTX, kv_heads, HD)
    value_four = value_rows.astype(jnp.float32).reshape(row_denominator_sum, CTX, kv_heads, HD)
    current_key = new_keys.astype(jnp.float32).reshape(row_denominator_sum, kv_heads, HD)
    own_value = new_values.astype(jnp.float32).reshape(row_denominator_sum, kv_heads, HD)
    scores = jnp.einsum('bkgd,bckd->bkgc', query_grouped_four, key_four) * attention_logit_scale
    positions = jnp.arange(CTX, dtype=jnp.int32)
    valid_mask = positions[None, :] < context_len[:, None]
    scores = jnp.where(valid_mask[:, None, None, :], scores, masked_score)
    current_score = jnp.einsum('cnhz,cnz->cnh', query_grouped_four, current_key) * attention_logit_scale
    row_max = jnp.maximum(lax.optimization_barrier(jnp.max(scores, axis=3)), current_score)
    exponent = jnp.exp(scores - row_max[..., None])
    own_exponent = jnp.exp(current_score - row_max)
    denominator = lax.optimization_barrier(jnp.sum(exponent, axis=3)) + own_exponent
    weights = lax.optimization_barrier((exponent / denominator[..., None]).astype(jnp.bfloat16)).astype(jnp.float32)
    own_weight = lax.optimization_barrier((own_exponent / denominator).astype(jnp.bfloat16)).astype(jnp.float32)
    combined = jnp.einsum('bkgc,bckd->bkgd', weights, value_four)
    combined = combined + own_weight[..., None] * own_value[:, :, None, :]
    return combined.reshape(row_denominator_sum, -1).astype(jnp.bfloat16)

def reference(queries, new_keys, new_values, key_cache, value_cache, context_len, cache_slot, residual_in, out_weight, gate_weight, up_weight):
    block_count = ROWS // ROWS_DEV

    def one_block(block_index):
        row_start = (block_index * ROWS_DEV).astype(jnp.int32)
        slot_rows = lax.dynamic_slice_in_dim(cache_slot, row_start, ROWS_DEV)
        key_rows = jnp.take(key_cache, slot_rows, axis=0)
        value_rows = jnp.take(value_cache, slot_rows, axis=0)
        return attend_block(lax.dynamic_slice_in_dim(queries, row_start, ROWS_DEV), lax.dynamic_slice_in_dim(new_keys, row_start, ROWS_DEV), lax.dynamic_slice_in_dim(new_values, row_start, ROWS_DEV), key_rows, value_rows, lax.dynamic_slice_in_dim(context_len, row_start, ROWS_DEV))
    attended = lax.map(one_block, jnp.arange(block_count, dtype=jnp.int32))
    attended = attended.reshape(ROWS, H * HD)
    output_projected = jnp.dot(attended, out_weight, preferred_element_type=jnp.float32)
    residual_out = (residual_in.astype(jnp.float32) + output_projected).astype(jnp.bfloat16)
    widened = lax.optimization_barrier(residual_out).astype(jnp.float32)
    squares = lax.optimization_barrier(jnp.sum(widened * widened, axis=1))
    inverse_rms = lax.rsqrt(squares / D + norm_epsilon)
    gate_value = jnp.dot(residual_out, gate_weight, preferred_element_type=jnp.float32) * inverse_rms[:, None]
    upward = jnp.dot(residual_out, up_weight, preferred_element_type=jnp.float32) * inverse_rms[:, None]
    activation = (jax.nn.silu(gate_value) * upward).astype(jnp.bfloat16)
    return (residual_out, activation)
```

```python
import functools
import itertools

import jax
import jax.numpy as jnp
from jax import lax
from jax.experimental import pallas as pl
from jax.experimental.pallas import tpu as pltpu
from jax.sharding import Mesh
from jax.sharding import PartitionSpec as P

D = 8192
HD = 128
EPS = 1e-05
MASKED = -1e30
BF = jnp.bfloat16
F32 = jnp.float32

FINE = ("g", "yl", "zh", "z1", "z0", "yh", "xh", "xl")
MC = ("yh", "xh", "xl")
KAPPA = ("yl", "zh", "z1")
YLZ = ("yl", "zh", "z1", "z0")


def dot(a, b, contract):
    return lax.dot_general(a, b, ((contract[0], contract[1]), ((), ())), preferred_element_type=F32)


def attend_kernel(slot_ref, len_ref, bit_ref, q_ref, nk_ref, nv_ref, k_hbm, v_hbm, a_ref, b_ref,
                  kbuf, vbuf, score, own, weight, own_weight, mixed, ksem, vsem):
    rows, context = kbuf.shape[0], kbuf.shape[1]
    heads = q_ref.shape[1] // HD

    def k_copy(r):
        return pltpu.make_async_copy(k_hbm.at[slot_ref[r]], kbuf.at[r], ksem.at[r])

    def v_copy(r):
        return pltpu.make_async_copy(v_hbm.at[slot_ref[r]], vbuf.at[r], vsem.at[r])

    for r in range(rows):
        k_copy(r).start()
    for r in range(rows):
        v_copy(r).start()
    scale = HD ** (-0.5)
    q = q_ref[...].astype(F32)
    nk = nk_ref[...].astype(F32)
    nv = nv_ref[...].astype(F32)
    position = lax.broadcasted_iota(jnp.int32, (heads, context), 1)
    group = 6
    for base in range(0, rows, group):
        for r in range(base, base + group):
            k_copy(r).wait()
        for r in range(base, base + group):
            q8 = jnp.concatenate(
                [q[r : r + 1, h * HD : (h + 1) * HD] for h in range(heads)], axis=0
            )
            s = dot(q8.astype(BF), kbuf[r], ((1,), (1,))) * scale
            score[r * heads : (r + 1) * heads, :] = jnp.where(position < len_ref[r], s, MASKED)
            mine = jnp.sum(q8 * nk[r : r + 1, :], axis=1, keepdims=True) * scale
            own[r * heads : (r + 1) * heads, :] = jnp.broadcast_to(mine, (heads, HD))
    s = score[...]
    mine = own[:, 0:1]
    top = jnp.maximum(jnp.max(s, axis=1, keepdims=True), mine)
    e = jnp.exp(s - top)
    own_e = jnp.exp(mine - top)
    total = jnp.sum(e, axis=1, keepdims=True) + own_e
    weight[...] = (e / total).astype(BF).astype(F32)
    own_weight[...] = jnp.broadcast_to((own_e / total).astype(BF).astype(F32), own_weight.shape)
    for base in range(0, rows, group):
        for r in range(base, base + group):
            v_copy(r).wait()
        for r in range(base, base + group):
            w = weight[r * heads : (r + 1) * heads, :].astype(BF)
            o = dot(w, vbuf[r], ((1,), (0,)))
            mixed[r] = o + own_weight[r * heads : (r + 1) * heads, :] * nv[r : r + 1, :]
    half_bit, quarter_bit = bit_ref[0], bit_ref[1]
    out = mixed[...]
    for h in range(heads):
        half, quarter, inner = h // 4, (h // 2) % 2, h % 2
        value = out[:, h, :].astype(BF)
        lanes = slice(inner * HD, (inner + 1) * HD)

        @pl.when(half == half_bit)
        def _(value=value, quarter=quarter, lanes=lanes):
            a_ref[jnp.bitwise_xor(quarter, quarter_bit), :, lanes] = value

        @pl.when(half != half_bit)
        def _(value=value, quarter=quarter, lanes=lanes):
            b_ref[jnp.bitwise_xor(quarter, quarter_bit), :, lanes] = value


def attend(slots, lens, bits, queries, new_keys, new_values, key_cache, value_cache):
    rows, context = key_cache.shape[0], key_cache.shape[1]
    heads = queries.shape[1] // HD
    smem = pl.BlockSpec(memory_space=pltpu.SMEM)
    vmem = pl.BlockSpec(memory_space=pltpu.VMEM)
    hbm = pl.BlockSpec(memory_space=pl.ANY)
    part = jax.ShapeDtypeStruct((2, rows, 2 * HD), BF)
    return pl.pallas_call(
        attend_kernel,
        out_shape=(part, part),
        in_specs=[smem, smem, smem, vmem, vmem, vmem, hbm, hbm],
        out_specs=(vmem, vmem),
        scratch_shapes=[
            pltpu.VMEM((rows, context, HD), BF),
            pltpu.VMEM((rows, context, HD), BF),
            pltpu.VMEM((rows * heads, context), F32),
            pltpu.VMEM((rows * heads, HD), F32),
            pltpu.VMEM((rows * heads, context), F32),
            pltpu.VMEM((rows * heads, HD), F32),
            pltpu.VMEM((rows, heads, HD), F32),
            pltpu.SemaphoreType.DMA((rows,)),
            pltpu.SemaphoreType.DMA((rows,)),
        ],
        compiler_params=pltpu.CompilerParams(vmem_limit_bytes=48 << 20),
        name="attend",
    )(slots, lens, bits, queries, new_keys, new_values, key_cache, value_cache)


def project_kernel(a_order, b_order, bit_ref, xa_ref, xb_ref, w00, w01, w10, w11, out_ref):
    parts, rows = out_ref.shape[0], out_ref.shape[1]

    def stack(ref, order, quarter):
        return jnp.concatenate([ref[order[p], quarter].astype(F32) for p in range(parts)], axis=0).astype(BF)

    swap = bit_ref[0]
    for first, second, when in ((( xa_ref, a_order), (xb_ref, b_order), 0), ((xb_ref, b_order), (xa_ref, a_order), 1)):
        @pl.when(swap == when)
        def _(first=first, second=second):
            total = dot(stack(*first, 0), w00[...], ((1,), (0,)))
            total += dot(stack(*first, 1), w01[...], ((1,), (0,)))
            total += dot(stack(*second, 0), w10[...], ((1,), (0,)))
            total += dot(stack(*second, 1), w11[...], ((1,), (0,)))
            out_ref[...] = total.reshape(parts, rows, total.shape[1]).astype(BF)


def project(bit, xa, xb, weights, a_order, b_order):
    parts, _, rows, _ = xa.shape
    vmem = pl.BlockSpec(memory_space=pltpu.VMEM)
    return pl.pallas_call(
        functools.partial(project_kernel, a_order, b_order),
        out_shape=jax.ShapeDtypeStruct((parts, rows, weights[0].shape[1]), BF),
        in_specs=[pl.BlockSpec(memory_space=pltpu.SMEM)] + [vmem] * 6,
        out_specs=vmem,
        compiler_params=pltpu.CompilerParams(vmem_limit_bytes=32 << 20),
        name="project",
    )(bit, xa, xb, *weights)


def join_kernel(parts_ref, residual_ref, out_ref, copies_ref):
    total = residual_ref[...].astype(F32)
    acc = parts_ref[0].astype(F32)
    for p in range(1, parts_ref.shape[0]):
        acc += parts_ref[p].astype(F32)
    total = (total + acc).astype(BF)
    out_ref[...] = total
    for c in range(copies_ref.shape[0]):
        copies_ref[c] = total


def join(parts, residual, copies):
    vmem = pl.BlockSpec(memory_space=pltpu.VMEM)
    return pl.pallas_call(
        join_kernel,
        out_shape=(
            jax.ShapeDtypeStruct(residual.shape, BF),
            jax.ShapeDtypeStruct((copies, *residual.shape), BF),
        ),
        in_specs=[vmem, vmem],
        out_specs=(vmem, vmem),
        name="join",
    )(parts, residual)


def expand_kernel(base_ref, x_ref, wg_ref, wu_ref, *rest):
    u_ref = rest[-2]
    held = rest[-1]
    c = pl.program_id(0)
    per_dest = held.shape[0] // 2

    @pl.when(c == 0)
    def _():
        x = x_ref[...].astype(F32)
        held[...] = x.reshape(held.shape).astype(BF)
        ones = jnp.ones((16, held.shape[1]), BF)
        for d in range(2):
            v = held[d * per_dest : (d + 1) * per_dest, :].astype(F32)
            square = v * v
            high = square.astype(BF)
            low = (square - high.astype(F32)).astype(BF)
            total = dot(ones, high, ((1,), (1,))) + dot(ones, low, ((1,), (1,)))
            upper = total.astype(BF).astype(F32)
            lower = total - upper
            line = lax.broadcasted_iota(jnp.int32, total.shape, 0)
            both = jnp.where(line == 0, upper, jnp.where(line == 1, lower, 0.0))
            tail = u_ref.shape[1] - 16
            u_ref[d, tail:, :] = jnp.zeros((16, HD), BF)
            u_ref[d, tail:, 0:per_dest] = both.astype(BF)

    w = jnp.concatenate([wg_ref[...], wu_ref[...]], axis=1)
    y = dot(held[...], w, ((1,), (0,))).astype(BF)
    start = pl.multiple_of(c * (2 * per_dest), 2 * per_dest)
    for d in range(2):
        mine = y[d * per_dest : (d + 1) * per_dest, :]
        u_ref[d, pl.ds(start, per_dest), :] = mine[:, :HD]
        u_ref[d, pl.ds(start + per_dest, per_dest), :] = mine[:, HD:]


def expand(base, x, wg, wu, so_far):
    parts, rows, depth = x.shape
    steps = wg.shape[1] // HD
    per_dest = parts * rows // 2
    height = steps * 2 * per_dest + 16
    specs = [
        pl.BlockSpec((parts, rows, depth), lambda c, base: (0, 0, 0)),
        pl.BlockSpec((depth, HD), lambda c, base: (0, c)),
        pl.BlockSpec((depth, HD), lambda c, base: (0, c)),
    ]
    args = [x, wg, wu]
    aliases = {}
    if so_far is not None:
        specs.append(pl.BlockSpec(memory_space=pl.ANY))
        args.append(so_far)
        aliases = {4: 0}
    return pl.pallas_call(
        expand_kernel,
        out_shape=jax.ShapeDtypeStruct((8, height, HD), BF),
        grid_spec=pltpu.PrefetchScalarGridSpec(
            num_scalar_prefetch=1,
            grid=(steps,),
            in_specs=specs,
            out_specs=pl.BlockSpec((2, height, HD), lambda c, base: (base[0], 0, 0)),
            scratch_shapes=[pltpu.VMEM((parts * rows, depth), BF)],
        ),
        input_output_aliases=aliases,
        compiler_params=pltpu.CompilerParams(vmem_limit_bytes=32 << 20),
        name="expand",
    )(base, *args)


def activate_kernel(u_ref, square_ref, out_ref, scale):
    per_dest = out_ref.shape[0]

    @pl.when(pl.program_id(0) == 0)
    def _():
        s = square_ref[0].astype(F32)
        for p in range(1, square_ref.shape[0]):
            s += square_ref[p].astype(F32)
        line = s[0:1, :] + s[1:2, :]
        square = jnp.broadcast_to(line, (HD, HD)).T
        scale[...] = lax.rsqrt(square[:per_dest, :] / D + EPS)

    total = u_ref[0].astype(F32)
    for p in range(1, u_ref.shape[0]):
        total += u_ref[p].astype(F32)
    gate = total[:per_dest] * scale[...]
    up = total[per_dest:] * scale[...]
    out_ref[...] = (gate / (1.0 + jnp.exp(-gate)) * up).astype(BF)


def activate(u, per_dest, columns):
    parts, height, _ = u.shape
    steps = columns // HD
    return pl.pallas_call(
        activate_kernel,
        out_shape=jax.ShapeDtypeStruct((per_dest, columns), BF),
        grid=(steps,),
        in_specs=[
            pl.BlockSpec((parts, 2 * per_dest, HD), lambda c: (0, c, 0)),
            pl.BlockSpec((parts, 16, HD), lambda c: (0, (height - 16) // 16, 0)),
        ],
        out_specs=pl.BlockSpec((per_dest, HD), lambda c: (0, c)),
        scratch_shapes=[pltpu.VMEM((per_dest, HD), F32)],
        name="activate",
    )(u, u)


def number(*bits):
    n = 0
    for b in bits:
        n = 2 * n + b
    return n


def partner_pairs(which):
    pairs = []
    for g, z0, a, b, c, d, e, f in itertools.product(range(2), repeat=8):
        half = d if which == 0 else 1 - d
        first = c if which == 0 else 1 - c
        pairs.append((number(g, a, b, c, z0, d, e, f), number(g, e, f, half, z0, first, a, b)))
    return pairs


def source_order(which):
    order = []
    for a, b, c in itertools.product(range(2), repeat=3):
        order.append(number(c if which == 0 else 1 - c, a, b))
    return tuple(order)


def swapped(x, axis):
    return lax.ppermute(x, axis, [(0, 1), (1, 0)])


def exchange(x, axes):
    return lax.all_to_all(x, axes, 0, 0, tiled=True)


def scalar(*values):
    return jnp.stack([jnp.asarray(v, jnp.int32) for v in values])


def body(queries, new_keys, new_values, key_cache, value_cache, context_len, cache_slot,
         residual_in, out_weight, gate_weight, up_weight):
    rows = queries.shape[0]
    g, yl, z1, z0, yh = (lax.axis_index(a) for a in ("g", "yl", "z1", "z0", "yh"))
    row_base = lax.axis_index(("g",) + YLZ) * rows

    w00 = out_weight
    w01 = swapped(out_weight, "z0")
    w10 = swapped(out_weight, "g")
    w11 = swapped(w01, "g")

    half_a, half_b = attend(cache_slot - row_base, context_len, scalar(yh, z0), queries, new_keys,
                            new_values, key_cache, value_cache)
    half_a = lax.ppermute(half_a, FINE, partner_pairs(0))
    half_b = lax.ppermute(half_b, FINE, partner_pairs(1))
    both = jnp.stack([half_a, half_b])
    spread = exchange(jnp.broadcast_to(both[None], (8, *both.shape)), MC)
    partial = project(scalar(jnp.bitwise_xor(g, z1)), spread[:, 0], spread[:, 1], (w00, w01, w10, w11),
                      source_order(0), source_order(1))
    residual_out, copies = join(exchange(partial, KAPPA), residual_in, 16)
    everyone = exchange(copies, YLZ)
    mine, theirs = everyone, swapped(everyone, "g")
    u = None
    for block, gg in ((mine, g), (theirs, 1 - g)):
        for part in range(2):
            u = expand(scalar(gg * 2 + part), block[8 * part : 8 * part + 8], gate_weight, up_weight, u)
    activation = activate(exchange(u, MC), 4 * rows, gate_weight.shape[1])
    return (residual_out, activation)


def solution(mesh):
    fine = Mesh(mesh.devices.reshape((2,) * 8), FINE)
    r = ("g",) + YLZ
    in_specs = (P(r, MC), P(r, MC), P(r, MC), P(r, None, MC), P(r, None, MC), P(r), P(r), P(r, MC),
                P(r, MC), P(MC, r), P(MC, r))
    out_specs = (P(r, MC), P(MC, r))
    return jax.shard_map(body, mesh=fine, in_specs=in_specs, out_specs=out_specs, check_vma=False)
```

```python
import functools

import jax
import jax.numpy as jnp
from jax import lax
from jax.experimental import pallas as pl
from jax.experimental.pallas import tpu as pltpu
from jax.sharding import Mesh
from jax.sharding import PartitionSpec as P

D = 8192
HD = 128
EPS = 1e-05
MASKED = -1e30
BF = jnp.bfloat16
F32 = jnp.float32

FINE = ("g", "yl", "zh", "z1", "z0", "yh", "xh", "xl")
MC = ("yh", "xh", "xl")
KAPPA = ("yl", "zh", "z1")
YLZ = ("yl", "zh", "z1", "z0")


def dot(a, b, contract):
    return lax.dot_general(a, b, ((contract[0], contract[1]), ((), ())), preferred_element_type=F32)


def in_hbm(x):
    return pltpu.with_memory_space_constraint(x, pltpu.HBM)


def attend_kernel(slot_hbm, len_hbm, q_hbm, nk_hbm, nv_hbm, k_hbm, v_hbm, out_ref,
                  slot, length, source, q_in, nk_in, nv_in, kbuf, vbuf, q3, nk, nv,
                  score, own, weight, own_weight, mixed, sems, ksem, vsem):
    rows, context = kbuf.shape[0], kbuf.shape[1]
    heads = q_in.shape[1] // HD
    group = rows // ksem.shape[0]

    def k_copy(i):
        part = pl.ds(i * group, group)
        return pltpu.make_async_copy(k_hbm.at[part], kbuf.at[part], ksem.at[i])

    def v_copy(i):
        part = pl.ds(i * group, group)
        return pltpu.make_async_copy(v_hbm.at[part], vbuf.at[part], vsem.at[i])

    small = [
        pltpu.make_async_copy(slot_hbm, slot, sems.at[0]),
        pltpu.make_async_copy(len_hbm, length, sems.at[1]),
        pltpu.make_async_copy(q_hbm, q_in, sems.at[2]),
        pltpu.make_async_copy(nk_hbm, nk_in, sems.at[3]),
        pltpu.make_async_copy(nv_hbm, nv_in, sems.at[4]),
    ]
    for copy in small:
        copy.start()
    for i in range(ksem.shape[0]):
        k_copy(i).start()
    for i in range(ksem.shape[0]):
        v_copy(i).start()
    for copy in small:
        copy.wait()
    for r in range(rows):
        source[lax.rem(slot[r], rows)] = r
    scale = HD ** (-0.5)
    for h in range(heads):
        q3[:, h, :] = q_in[:, h * HD : (h + 1) * HD].astype(F32)
    nk[...] = nk_in[...].astype(F32)
    nv[...] = nv_in[...].astype(F32)
    position = lax.broadcasted_iota(jnp.int32, (heads, context), 1)
    for i in range(ksem.shape[0]):
        k_copy(i).wait()
        for s in range(i * group, (i + 1) * group):
            r = source[s]
            q8 = q3[r]
            line = slice(s * heads, (s + 1) * heads)
            logits = dot(q8.astype(BF), kbuf[s], ((1,), (1,))) * scale
            score[line, :] = jnp.where(position < length[r], logits, MASKED)
            mine = jnp.sum(q8 * nk[pl.ds(r, 1), :], axis=1, keepdims=True) * scale
            own[line, :] = jnp.broadcast_to(mine, (heads, HD))
    logits = score[...]
    mine = own[:, 0:1]
    top = jnp.maximum(jnp.max(logits, axis=1, keepdims=True), mine)
    e = jnp.exp(logits - top)
    own_e = jnp.exp(mine - top)
    total = jnp.sum(e, axis=1, keepdims=True) + own_e
    weight[...] = (e / total).astype(BF)
    own_weight[...] = jnp.broadcast_to((own_e / total).astype(BF).astype(F32), own_weight.shape)
    for i in range(ksem.shape[0]):
        v_copy(i).wait()
        for s in range(i * group, (i + 1) * group):
            r = source[s]
            line = slice(s * heads, (s + 1) * heads)
            o = dot(weight[line, :], vbuf[s], ((1,), (0,)))
            mixed[r] = o + own_weight[line, :] * nv[pl.ds(r, 1), :]
    z0 = lax.axis_index("z0")
    for half in range(2):
        pairs = []
        for quarter in range(2):
            h = 4 * half + 2 * quarter
            pairs.append(jnp.concatenate([mixed[:, h, :], mixed[:, h + 1, :]], axis=1).astype(BF))
        first = jnp.where(z0 == 0, pairs[0], pairs[1])
        second = jnp.where(z0 == 0, pairs[1], pairs[0])
        value = jnp.concatenate([first, second], axis=1)
        for c in range(out_ref.shape[0]):
            out_ref[c, half] = value


def attend(copies, slots, lens, queries, new_keys, new_values, key_cache, value_cache):
    rows, context = key_cache.shape[0], key_cache.shape[1]
    heads = queries.shape[1] // HD
    chunks = 4
    hbm = pl.BlockSpec(memory_space=pltpu.HBM)
    return pl.pallas_call(
        attend_kernel,
        out_shape=jax.ShapeDtypeStruct((copies, 2, rows, heads // 2 * HD), BF),
        in_specs=[hbm] * 7,
        out_specs=pl.BlockSpec(memory_space=pltpu.VMEM),
        scratch_shapes=[
            pltpu.SMEM((rows,), jnp.int32),
            pltpu.SMEM((rows,), jnp.int32),
            pltpu.SMEM((rows,), jnp.int32),
            pltpu.VMEM(queries.shape, BF),
            pltpu.VMEM(new_keys.shape, BF),
            pltpu.VMEM(new_values.shape, BF),
            pltpu.VMEM((rows, context, HD), BF),
            pltpu.VMEM((rows, context, HD), BF),
            pltpu.VMEM((rows, heads, HD), F32),
            pltpu.VMEM((rows, HD), F32),
            pltpu.VMEM((rows, HD), F32),
            pltpu.VMEM((rows * heads, context), F32),
            pltpu.VMEM((rows * heads, HD), F32),
            pltpu.VMEM((rows * heads, context), BF),
            pltpu.VMEM((rows * heads, HD), F32),
            pltpu.VMEM((rows, heads, HD), F32),
            pltpu.SemaphoreType.DMA((5,)),
            pltpu.SemaphoreType.DMA((chunks,)),
            pltpu.SemaphoreType.DMA((chunks,)),
        ],
        compiler_params=pltpu.CompilerParams(vmem_limit_bytes=48 << 20),
        name="attend",
    )(*map(in_hbm, (slots, lens, queries, new_keys, new_values, key_cache, value_cache)))


def project_kernel(x_ref, w00, w01, w10, w11, out_ref):
    parts, rows = out_ref.shape[0], out_ref.shape[1]
    g = lax.axis_index("g")

    def stack(side):
        return jnp.concatenate([x_ref[p, side].astype(F32) for p in range(parts)], axis=0).astype(BF)

    mine, theirs = stack(g), stack(1 - g)
    half = w00.shape[0]
    total = dot(mine[:, :half], w00[...], ((1,), (0,)))
    total += dot(mine[:, half:], w01[...], ((1,), (0,)))
    total += dot(theirs[:, :half], w10[...], ((1,), (0,)))
    total += dot(theirs[:, half:], w11[...], ((1,), (0,)))
    out_ref[...] = total.reshape(parts, rows, total.shape[1]).astype(BF)


def project(x, weights):
    parts, _, rows, _ = x.shape
    vmem = pl.BlockSpec(memory_space=pltpu.VMEM)
    return pl.pallas_call(
        project_kernel,
        out_shape=jax.ShapeDtypeStruct((parts, rows, weights[0].shape[1]), BF),
        in_specs=[vmem] * 5,
        out_specs=vmem,
        compiler_params=pltpu.CompilerParams(vmem_limit_bytes=32 << 20),
        name="project",
    )(x, *weights)


def join_kernel(parts_ref, residual_ref, out_ref, copies_ref):
    total = residual_ref[...].astype(F32)
    acc = parts_ref[0].astype(F32)
    for p in range(1, parts_ref.shape[0]):
        acc += parts_ref[p].astype(F32)
    total = (total + acc).astype(BF)
    out_ref[...] = total
    for c in range(copies_ref.shape[0]):
        copies_ref[c] = total


def join(parts, residual, copies):
    vmem = pl.BlockSpec(memory_space=pltpu.VMEM)
    return pl.pallas_call(
        join_kernel,
        out_shape=(
            jax.ShapeDtypeStruct(residual.shape, BF),
            jax.ShapeDtypeStruct((copies, *residual.shape), BF),
        ),
        in_specs=[vmem, vmem],
        out_specs=(vmem, vmem),
        name="join",
    )(parts, residual)


TAIL = 16


def expand_kernel(first_ref, x_ref, wg_hbm, wu_hbm, *rest):
    u_hbm, wg, wu, held, staged, wsem, usem = rest[-7:]
    dests, height = staged.shape[0], staged.shape[1]
    per_dest = held.shape[0] // dests
    end = height - TAIL
    copies = [
        pltpu.make_async_copy(wg_hbm, wg, wsem.at[0]),
        pltpu.make_async_copy(wu_hbm, wu, wsem.at[1]),
    ]
    for copy in copies:
        copy.start()

    x = x_ref[...].astype(F32).reshape(held.shape)
    held[...] = x.astype(BF)
    folded = jnp.zeros((held.shape[0], HD), F32)
    for t in range(held.shape[1] // HD):
        v = x[:, t * HD : (t + 1) * HD]
        folded += v * v
    upper = folded.astype(BF)
    lower = (folded - upper.astype(F32)).astype(BF)
    ones = jnp.ones((TAIL, HD), BF)
    for d in range(dests):
        part = slice(d * per_dest, (d + 1) * per_dest)
        total = dot(ones, upper[part], ((1,), (1,))) + dot(ones, lower[part], ((1,), (1,)))
        top = total.astype(BF).astype(F32)
        line = lax.broadcasted_iota(jnp.int32, total.shape, 0)
        both = jnp.where(line == 0, top, jnp.where(line == 1, total - top, 0.0))
        staged[d, end:, :] = jnp.zeros((TAIL, HD), BF)
        staged[d, end:, 0:per_dest] = both.astype(BF)

    for w, copy, shift in ((wg, copies[0], 0), (wu, copies[1], per_dest)):
        copy.wait()
        for lane in range(0, w.shape[1], 2 * HD):
            width = min(2 * HD, w.shape[1] - lane)
            y = dot(held[...], w[:, lane : lane + width], ((1,), (0,))).astype(BF)
            for c in range(width // HD):
                row = (lane // HD + c) * 2 * per_dest + shift
                for d in range(dests):
                    staged[d, row : row + per_dest, :] = y[d * per_dest : (d + 1) * per_dest, c * HD : (c + 1) * HD]
    out = pltpu.make_async_copy(staged, u_hbm.at[pl.ds(first_ref[0] * dests, dests)], usem)
    out.start()
    out.wait()


def expand(first, x, wg, wu, so_far):
    parts, rows, depth = x.shape
    dests = 4
    per_dest = parts * rows // dests
    height = wg.shape[1] // HD * 2 * per_dest + TAIL
    hbm = pl.BlockSpec(memory_space=pltpu.HBM)
    specs = [pl.BlockSpec(memory_space=pltpu.SMEM), pl.BlockSpec(memory_space=pltpu.VMEM), hbm, hbm]
    args = [first, x, in_hbm(wg), in_hbm(wu)]
    aliases = {}
    if so_far is not None:
        specs.append(hbm)
        args.append(so_far)
        aliases = {4: 0}
    return pl.pallas_call(
        expand_kernel,
        out_shape=jax.ShapeDtypeStruct((8, height, HD), BF),
        in_specs=specs,
        out_specs=hbm,
        scratch_shapes=[
            pltpu.VMEM(wg.shape, BF),
            pltpu.VMEM(wu.shape, BF),
            pltpu.VMEM((parts * rows, depth), BF),
            pltpu.VMEM((dests, height, HD), BF),
            pltpu.SemaphoreType.DMA((2,)),
            pltpu.SemaphoreType.DMA,
        ],
        input_output_aliases=aliases,
        compiler_params=pltpu.CompilerParams(vmem_limit_bytes=32 << 20),
        name="expand",
    )(*args)


def activate_kernel(u_ref, out_ref):
    per_dest = out_ref.shape[0]
    end = u_ref.shape[1] - TAIL
    s = u_ref[0, end:, :].astype(F32)
    for p in range(1, u_ref.shape[0]):
        s += u_ref[p, end:, :].astype(F32)
    square = jnp.broadcast_to(s[0:1, :] + s[1:2, :], (HD, HD)).T
    scale = lax.rsqrt(square[:per_dest, :] / D + EPS)
    for c in range(end // (2 * per_dest)):
        start = c * 2 * per_dest
        total = u_ref[0, start : start + 2 * per_dest].astype(F32)
        for p in range(1, u_ref.shape[0]):
            total += u_ref[p, start : start + 2 * per_dest].astype(F32)
        gate = total[:per_dest] * scale
        up = total[per_dest:] * scale
        out_ref[:, c * HD : (c + 1) * HD] = (gate / (1.0 + jnp.exp(-gate)) * up).astype(BF)


def activate(u, per_dest):
    columns = (u.shape[1] - TAIL) // (2 * per_dest) * HD
    vmem = pl.BlockSpec(memory_space=pltpu.VMEM)
    return pl.pallas_call(
        activate_kernel,
        out_shape=jax.ShapeDtypeStruct((per_dest, columns), BF),
        in_specs=[vmem],
        out_specs=vmem,
        compiler_params=pltpu.CompilerParams(vmem_limit_bytes=32 << 20),
        name="activate",
    )(u)


def swapped(x, axis):
    return lax.ppermute(x, axis, [(0, 1), (1, 0)])


def exchange(x, axes):
    return lax.all_to_all(x, axes, 0, 0, tiled=True)


def scalar(*values):
    return jnp.stack([jnp.asarray(v, jnp.int32) for v in values])


def body(queries, new_keys, new_values, key_cache, value_cache, context_len, cache_slot,
         residual_in, out_weight, gate_weight, up_weight):
    rows = queries.shape[0]
    g = lax.axis_index("g")

    w01 = swapped(out_weight, "z0")
    w10 = swapped(out_weight, "g")
    w11 = swapped(w01, "g")

    attended = attend(8, cache_slot, context_len, queries, new_keys, new_values, key_cache, value_cache)
    attended, w10 = lax.optimization_barrier((attended, w10))
    heads = exchange(attended, MC)
    heads = heads.reshape(2, 4, *heads.shape[1:]).transpose(1, 2, 0, 3, 4)
    heads = heads.reshape(8, *heads.shape[2:])
    partial = project(exchange(heads, KAPPA), (out_weight, w01, w10, w11))
    residual_out, copies = join(exchange(partial, KAPPA), residual_in, 16)
    mine = exchange(copies, YLZ)
    theirs = swapped(mine, "g")
    u = expand(scalar(g), mine, gate_weight, up_weight, None)
    u = expand(scalar(1 - g), theirs, gate_weight, up_weight, u)
    activation = activate(exchange(u, MC), 4 * rows)
    return (residual_out, activation)


def solution(mesh):
    fine = Mesh(mesh.devices.reshape((2,) * 8), FINE)
    r = ("g",) + YLZ
    in_specs = (P(r, MC), P(r, MC), P(r, MC), P(r, None, MC), P(r, None, MC), P(r), P(r), P(r, MC),
                P(r, MC), P(MC, r), P(MC, r))
    out_specs = (P(r, MC), P(MC, r))
    return jax.shard_map(body, mesh=fine, in_specs=in_specs, out_specs=out_specs, check_vma=False)
```

```python
import functools

import jax
import jax.numpy as jnp
from jax import lax
from jax.experimental import pallas as pl
from jax.experimental.pallas import tpu as pltpu
from jax.sharding import Mesh
from jax.sharding import PartitionSpec as P

D = 8192
HD = 128
EPS = 1e-05
MASKED = -1e30
BF = jnp.bfloat16
F32 = jnp.float32

FINE = ("g", "yl", "zh", "z1", "z0", "yh", "xh", "xl")
MC = ("yh", "xh", "xl")
KAPPA = ("yl", "zh", "z1")
YLZ = ("yl", "zh", "z1", "z0")


def dot(a, b, contract):
    return lax.dot_general(a, b, ((contract[0], contract[1]), ((), ())), preferred_element_type=F32)


def in_hbm(x):
    return pltpu.with_memory_space_constraint(x, pltpu.HBM)


def attend_kernel(slot_hbm, len_hbm, q_hbm, nk_hbm, nv_hbm, k_hbm, v_hbm, out_ref,
                  slot, length, source, q_in, nk_in, nv_in, kbuf, vbuf, q3, nk, nv,
                  score, own, weight, own_weight, mixed, sems, ksem, vsem):
    rows, context = kbuf.shape[0], kbuf.shape[1]
    heads = q_in.shape[1] // HD
    group = rows // ksem.shape[0]

    def k_copy(i):
        part = pl.ds(i * group, group)
        return pltpu.make_async_copy(k_hbm.at[part], kbuf.at[part], ksem.at[i])

    def v_copy(i):
        part = pl.ds(i * group, group)
        return pltpu.make_async_copy(v_hbm.at[part], vbuf.at[part], vsem.at[i])

    small = [
        pltpu.make_async_copy(slot_hbm, slot, sems.at[0]),
        pltpu.make_async_copy(len_hbm, length, sems.at[1]),
        pltpu.make_async_copy(q_hbm, q_in, sems.at[2]),
        pltpu.make_async_copy(nk_hbm, nk_in, sems.at[3]),
        pltpu.make_async_copy(nv_hbm, nv_in, sems.at[4]),
    ]
    for copy in small:
        copy.start()
    for i in range(ksem.shape[0]):
        k_copy(i).start()
    for copy in small:
        copy.wait()
    for r in range(rows):
        source[lax.rem(slot[r], rows)] = r
    scale = HD ** (-0.5)
    for h in range(heads):
        q3[:, h, :] = q_in[:, h * HD : (h + 1) * HD].astype(F32)
    nk[...] = nk_in[...].astype(F32)
    nv[...] = nv_in[...].astype(F32)
    position = lax.broadcasted_iota(jnp.int32, (heads, context), 1)
    for i in range(ksem.shape[0]):
        k_copy(i).wait()
        v_copy(i).start()
        for s in range(i * group, (i + 1) * group):
            r = source[s]
            q8 = q3[r]
            line = slice(s * heads, (s + 1) * heads)
            logits = dot(q8.astype(BF), kbuf[s], ((1,), (1,))) * scale
            score[line, :] = jnp.where(position < length[r], logits, MASKED)
            mine = jnp.sum(q8 * nk[pl.ds(r, 1), :], axis=1, keepdims=True) * scale
            own[line, :] = jnp.broadcast_to(mine, (heads, HD))
    logits = score[...]
    mine = own[:, 0:1]
    top = jnp.maximum(jnp.max(logits, axis=1, keepdims=True), mine)
    e = jnp.exp(logits - top)
    own_e = jnp.exp(mine - top)
    total = jnp.sum(e, axis=1, keepdims=True) + own_e
    weight[...] = (e / total).astype(BF)
    own_weight[...] = jnp.broadcast_to((own_e / total).astype(BF).astype(F32), own_weight.shape)
    for i in range(ksem.shape[0]):
        v_copy(i).wait()
        for s in range(i * group, (i + 1) * group):
            r = source[s]
            line = slice(s * heads, (s + 1) * heads)
            o = dot(weight[line, :], vbuf[s], ((1,), (0,)))
            mixed[r] = o + own_weight[line, :] * nv[pl.ds(r, 1), :]
    z0 = lax.axis_index("z0")
    for half in range(2):
        pairs = []
        for quarter in range(2):
            h = 4 * half + 2 * quarter
            pairs.append(jnp.concatenate([mixed[:, h, :], mixed[:, h + 1, :]], axis=1).astype(BF))
        first = jnp.where(z0 == 0, pairs[0], pairs[1])
        second = jnp.where(z0 == 0, pairs[1], pairs[0])
        value = jnp.concatenate([first, second], axis=1)
        for c in range(out_ref.shape[0]):
            out_ref[c, half] = value


def attend(copies, slots, lens, queries, new_keys, new_values, key_cache, value_cache):
    rows, context = key_cache.shape[0], key_cache.shape[1]
    heads = queries.shape[1] // HD
    chunks = 4
    hbm = pl.BlockSpec(memory_space=pltpu.HBM)
    return pl.pallas_call(
        attend_kernel,
        out_shape=jax.ShapeDtypeStruct((copies, 2, rows, heads // 2 * HD), BF),
        in_specs=[hbm] * 7,
        out_specs=pl.BlockSpec(memory_space=pltpu.VMEM),
        scratch_shapes=[
            pltpu.SMEM((rows,), jnp.int32),
            pltpu.SMEM((rows,), jnp.int32),
            pltpu.SMEM((rows,), jnp.int32),
            pltpu.VMEM(queries.shape, BF),
            pltpu.VMEM(new_keys.shape, BF),
            pltpu.VMEM(new_values.shape, BF),
            pltpu.VMEM((rows, context, HD), BF),
            pltpu.VMEM((rows, context, HD), BF),
            pltpu.VMEM((rows, heads, HD), F32),
            pltpu.VMEM((rows, HD), F32),
            pltpu.VMEM((rows, HD), F32),
            pltpu.VMEM((rows * heads, context), F32),
            pltpu.VMEM((rows * heads, HD), F32),
            pltpu.VMEM((rows * heads, context), BF),
            pltpu.VMEM((rows * heads, HD), F32),
            pltpu.VMEM((rows, heads, HD), F32),
            pltpu.SemaphoreType.DMA((5,)),
            pltpu.SemaphoreType.DMA((chunks,)),
            pltpu.SemaphoreType.DMA((chunks,)),
        ],
        compiler_params=pltpu.CompilerParams(vmem_limit_bytes=48 << 20),
        name="attend",
    )(*map(in_hbm, (slots, lens, queries, new_keys, new_values, key_cache, value_cache)))


def project_kernel(x_ref, w00, w01, w10, w11, out_ref):
    parts, rows = out_ref.shape[0], out_ref.shape[1]
    g = lax.axis_index("g")

    def stack(side):
        return jnp.concatenate([x_ref[p, side].astype(F32) for p in range(parts)], axis=0).astype(BF)

    mine, theirs = stack(g), stack(1 - g)
    half = w00.shape[0]
    total = dot(mine[:, :half], w00[...], ((1,), (0,)))
    total += dot(mine[:, half:], w01[...], ((1,), (0,)))
    total += dot(theirs[:, :half], w10[...], ((1,), (0,)))
    total += dot(theirs[:, half:], w11[...], ((1,), (0,)))
    out_ref[...] = total.reshape(parts, rows, total.shape[1]).astype(BF)


def project(x, weights):
    parts, _, rows, _ = x.shape
    vmem = pl.BlockSpec(memory_space=pltpu.VMEM)
    return pl.pallas_call(
        project_kernel,
        out_shape=jax.ShapeDtypeStruct((parts, rows, weights[0].shape[1]), BF),
        in_specs=[vmem] * 5,
        out_specs=vmem,
        compiler_params=pltpu.CompilerParams(vmem_limit_bytes=32 << 20),
        name="project",
    )(x, *weights)


def join_kernel(parts_ref, residual_ref, out_ref, copies_ref):
    total = residual_ref[...].astype(F32)
    acc = parts_ref[0].astype(F32)
    for p in range(1, parts_ref.shape[0]):
        acc += parts_ref[p].astype(F32)
    total = (total + acc).astype(BF)
    out_ref[...] = total
    for c in range(copies_ref.shape[0]):
        copies_ref[c] = total


def join(parts, residual, copies):
    vmem = pl.BlockSpec(memory_space=pltpu.VMEM)
    return pl.pallas_call(
        join_kernel,
        out_shape=(
            jax.ShapeDtypeStruct(residual.shape, BF),
            jax.ShapeDtypeStruct((copies, *residual.shape), BF),
        ),
        in_specs=[vmem, vmem],
        out_specs=(vmem, vmem),
        name="join",
    )(parts, residual)


TAIL = 16


def expand_kernel(first_ref, x_ref, wg_hbm, wu_hbm, *rest):
    u_hbm, wg, wu, held, staged, wsem, usem = rest[-7:]
    dests, height = staged.shape[0], staged.shape[1]
    per_dest = held.shape[0] // dests
    end = height - TAIL
    copies = [
        pltpu.make_async_copy(wg_hbm, wg, wsem.at[0]),
        pltpu.make_async_copy(wu_hbm, wu, wsem.at[1]),
    ]
    for copy in copies:
        copy.start()

    x = x_ref[...].astype(F32).reshape(held.shape)
    held[...] = x.astype(BF)
    folded = jnp.zeros((held.shape[0], HD), F32)
    for t in range(held.shape[1] // HD):
        v = x[:, t * HD : (t + 1) * HD]
        folded += v * v
    upper = folded.astype(BF)
    lower = (folded - upper.astype(F32)).astype(BF)
    ones = jnp.ones((TAIL, HD), BF)
    for d in range(dests):
        part = slice(d * per_dest, (d + 1) * per_dest)
        total = dot(ones, upper[part], ((1,), (1,))) + dot(ones, lower[part], ((1,), (1,)))
        top = total.astype(BF).astype(F32)
        line = lax.broadcasted_iota(jnp.int32, total.shape, 0)
        both = jnp.where(line == 0, top, jnp.where(line == 1, total - top, 0.0))
        staged[d, end:, :] = jnp.zeros((TAIL, HD), BF)
        staged[d, end:, 0:per_dest] = both.astype(BF)

    for w, copy, shift in ((wg, copies[0], 0), (wu, copies[1], per_dest)):
        copy.wait()
        for lane in range(0, w.shape[1], 2 * HD):
            width = min(2 * HD, w.shape[1] - lane)
            y = dot(held[...], w[:, lane : lane + width], ((1,), (0,))).astype(BF)
            for c in range(width // HD):
                row = (lane // HD + c) * 2 * per_dest + shift
                for d in range(dests):
                    staged[d, row : row + per_dest, :] = y[d * per_dest : (d + 1) * per_dest, c * HD : (c + 1) * HD]
    out = pltpu.make_async_copy(staged, u_hbm.at[pl.ds(first_ref[0] * dests, dests)], usem)
    out.start()
    out.wait()


def expand(first, x, wg, wu, so_far):
    parts, rows, depth = x.shape
    dests = 4
    per_dest = parts * rows // dests
    height = wg.shape[1] // HD * 2 * per_dest + TAIL
    hbm = pl.BlockSpec(memory_space=pltpu.HBM)
    specs = [pl.BlockSpec(memory_space=pltpu.SMEM), pl.BlockSpec(memory_space=pltpu.VMEM), hbm, hbm]
    args = [first, x, in_hbm(wg), in_hbm(wu)]
    aliases = {}
    if so_far is not None:
        specs.append(hbm)
        args.append(so_far)
        aliases = {4: 0}
    return pl.pallas_call(
        expand_kernel,
        out_shape=jax.ShapeDtypeStruct((8, height, HD), BF),
        in_specs=specs,
        out_specs=hbm,
        scratch_shapes=[
            pltpu.VMEM(wg.shape, BF),
            pltpu.VMEM(wu.shape, BF),
            pltpu.VMEM((parts * rows, depth), BF),
            pltpu.VMEM((dests, height, HD), BF),
            pltpu.SemaphoreType.DMA((2,)),
            pltpu.SemaphoreType.DMA,
        ],
        input_output_aliases=aliases,
        compiler_params=pltpu.CompilerParams(vmem_limit_bytes=32 << 20),
        name="expand",
    )(*args)


def activate_kernel(u_ref, out_ref):
    per_dest = out_ref.shape[0]
    end = u_ref.shape[1] - TAIL
    s = u_ref[0, end:, :].astype(F32)
    for p in range(1, u_ref.shape[0]):
        s += u_ref[p, end:, :].astype(F32)
    square = jnp.broadcast_to(s[0:1, :] + s[1:2, :], (HD, HD)).T
    scale = lax.rsqrt(square[:per_dest, :] / D + EPS)
    for c in range(end // (2 * per_dest)):
        start = c * 2 * per_dest
        total = u_ref[0, start : start + 2 * per_dest].astype(F32)
        for p in range(1, u_ref.shape[0]):
            total += u_ref[p, start : start + 2 * per_dest].astype(F32)
        gate = total[:per_dest] * scale
        up = total[per_dest:] * scale
        out_ref[:, c * HD : (c + 1) * HD] = (gate / (1.0 + jnp.exp(-gate)) * up).astype(BF)


def activate(u, per_dest):
    columns = (u.shape[1] - TAIL) // (2 * per_dest) * HD
    vmem = pl.BlockSpec(memory_space=pltpu.VMEM)
    return pl.pallas_call(
        activate_kernel,
        out_shape=jax.ShapeDtypeStruct((per_dest, columns), BF),
        in_specs=[vmem],
        out_specs=vmem,
        compiler_params=pltpu.CompilerParams(vmem_limit_bytes=32 << 20),
        name="activate",
    )(u)


def swapped(x, axis):
    return lax.ppermute(x, axis, [(0, 1), (1, 0)])


def exchange(x, axes):
    return lax.all_to_all(x, axes, 0, 0, tiled=True)


def scalar(*values):
    return jnp.stack([jnp.asarray(v, jnp.int32) for v in values])


def body(queries, new_keys, new_values, key_cache, value_cache, context_len, cache_slot,
         residual_in, out_weight, gate_weight, up_weight):
    rows = queries.shape[0]
    g = lax.axis_index("g")

    attended = attend(8, cache_slot, context_len, queries, new_keys, new_values, key_cache, value_cache)
    attended, out_weight = lax.optimization_barrier((attended, out_weight))
    w01 = swapped(out_weight, "z0")
    heads, w01, late = lax.optimization_barrier((exchange(attended, MC), w01, out_weight))
    w10 = swapped(late, "g")
    w11 = swapped(w01, "g")
    heads = heads.reshape(2, 4, *heads.shape[1:]).transpose(1, 2, 0, 3, 4)
    heads = heads.reshape(8, *heads.shape[2:])
    partial = project(exchange(heads, KAPPA), (out_weight, w01, w10, w11))
    residual_out, copies = join(exchange(partial, KAPPA), residual_in, 16)
    mine = exchange(copies, YLZ)
    theirs = swapped(mine, "g")
    u = expand(scalar(g), mine, gate_weight, up_weight, None)
    u = expand(scalar(1 - g), theirs, gate_weight, up_weight, u)
    activation = activate(exchange(u, MC), 4 * rows)
    return (residual_out, activation)


def solution(mesh):
    fine = Mesh(mesh.devices.reshape((2,) * 8), FINE)
    r = ("g",) + YLZ
    in_specs = (P(r, MC), P(r, MC), P(r, MC), P(r, None, MC), P(r, None, MC), P(r), P(r), P(r, MC),
                P(r, MC), P(MC, r), P(MC, r))
    out_specs = (P(r, MC), P(MC, r))
    return jax.shard_map(body, mesh=fine, in_specs=in_specs, out_specs=out_specs, check_vma=False)
```

```python
import functools

import jax
import jax.numpy as jnp
from jax import lax
from jax.experimental import pallas as pl
from jax.experimental.pallas import tpu as pltpu
from jax.sharding import Mesh
from jax.sharding import PartitionSpec as P

D = 8192
HD = 128
EPS = 1e-05
MASKED = -1e30
BF = jnp.bfloat16
F32 = jnp.float32

FINE = ("g", "yl", "zh", "z1", "z0", "yh", "xh", "xl")
MC = ("yh", "xh", "xl")
KAPPA = ("yl", "zh", "z1")
YLZ = ("yl", "zh", "z1", "z0")


def dot(a, b, contract):
    return lax.dot_general(a, b, ((contract[0], contract[1]), ((), ())), preferred_element_type=F32)


def in_hbm(x):
    return pltpu.with_memory_space_constraint(x, pltpu.HBM)


def attend_kernel(slot_hbm, len_hbm, q_hbm, nk_hbm, nv_hbm, k_hbm, v_hbm, out_ref,
                  slot, length, source, q_in, nk_in, nv_in, kbuf, vbuf, q3, nk, nv,
                  score, own, weight, own_weight, mixed, sems, ksem, vsem):
    rows, context = kbuf.shape[0], kbuf.shape[1]
    heads = q_in.shape[1] // HD
    group = rows // ksem.shape[0]

    def k_copy(i):
        part = pl.ds(i * group, group)
        return pltpu.make_async_copy(k_hbm.at[part], kbuf.at[part], ksem.at[i])

    def v_copy(i):
        part = pl.ds(i * group, group)
        return pltpu.make_async_copy(v_hbm.at[part], vbuf.at[part], vsem.at[i])

    small = [
        pltpu.make_async_copy(slot_hbm, slot, sems.at[0]),
        pltpu.make_async_copy(len_hbm, length, sems.at[1]),
        pltpu.make_async_copy(q_hbm, q_in, sems.at[2]),
        pltpu.make_async_copy(nk_hbm, nk_in, sems.at[3]),
        pltpu.make_async_copy(nv_hbm, nv_in, sems.at[4]),
    ]
    for copy in small:
        copy.start()
    for i in range(ksem.shape[0]):
        k_copy(i).start()
    for copy in small:
        copy.wait()
    for r in range(rows):
        source[lax.rem(slot[r], rows)] = r
    scale = HD ** (-0.5)
    for h in range(heads):
        q3[:, h, :] = q_in[:, h * HD : (h + 1) * HD].astype(F32)
    nk[...] = nk_in[...].astype(F32)
    nv[...] = nv_in[...].astype(F32)
    position = lax.broadcasted_iota(jnp.int32, (heads, context), 1)
    for i in range(ksem.shape[0]):
        k_copy(i).wait()
        v_copy(i).start()
        for s in range(i * group, (i + 1) * group):
            r = source[s]
            q8 = q3[r]
            line = slice(s * heads, (s + 1) * heads)
            logits = dot(q8.astype(BF), kbuf[s], ((1,), (1,))) * scale
            score[line, :] = jnp.where(position < length[r], logits, MASKED)
            mine = jnp.sum(q8 * nk[pl.ds(r, 1), :], axis=1, keepdims=True) * scale
            own[line, :] = jnp.broadcast_to(mine, (heads, HD))
    logits = score[...]
    mine = own[:, 0:1]
    top = jnp.maximum(jnp.max(logits, axis=1, keepdims=True), mine)
    e = jnp.exp(logits - top)
    own_e = jnp.exp(mine - top)
    total = jnp.sum(e, axis=1, keepdims=True) + own_e
    weight[...] = (e / total).astype(BF)
    own_weight[...] = jnp.broadcast_to((own_e / total).astype(BF).astype(F32), own_weight.shape)
    for i in range(ksem.shape[0]):
        v_copy(i).wait()
        for s in range(i * group, (i + 1) * group):
            r = source[s]
            line = slice(s * heads, (s + 1) * heads)
            o = dot(weight[line, :], vbuf[s], ((1,), (0,)))
            mixed[r] = o + own_weight[line, :] * nv[pl.ds(r, 1), :]
    z0 = lax.axis_index("z0")
    for half in range(2):
        pairs = []
        for quarter in range(2):
            h = 4 * half + 2 * quarter
            pairs.append(jnp.concatenate([mixed[:, h, :], mixed[:, h + 1, :]], axis=1).astype(BF))
        first = jnp.where(z0 == 0, pairs[0], pairs[1])
        second = jnp.where(z0 == 0, pairs[1], pairs[0])
        value = jnp.concatenate([first, second], axis=1)
        for c in range(out_ref.shape[0]):
            out_ref[c, half] = value


def attend(copies, slots, lens, queries, new_keys, new_values, key_cache, value_cache):
    rows, context = key_cache.shape[0], key_cache.shape[1]
    heads = queries.shape[1] // HD
    chunks = 4
    hbm = pl.BlockSpec(memory_space=pltpu.HBM)
    return pl.pallas_call(
        attend_kernel,
        out_shape=jax.ShapeDtypeStruct((copies, 2, rows, heads // 2 * HD), BF),
        in_specs=[hbm] * 7,
        out_specs=pl.BlockSpec(memory_space=pltpu.VMEM),
        scratch_shapes=[
            pltpu.SMEM((rows,), jnp.int32),
            pltpu.SMEM((rows,), jnp.int32),
            pltpu.SMEM((rows,), jnp.int32),
            pltpu.VMEM(queries.shape, BF),
            pltpu.VMEM(new_keys.shape, BF),
            pltpu.VMEM(new_values.shape, BF),
            pltpu.VMEM((rows, context, HD), BF),
            pltpu.VMEM((rows, context, HD), BF),
            pltpu.VMEM((rows, heads, HD), F32),
            pltpu.VMEM((rows, HD), F32),
            pltpu.VMEM((rows, HD), F32),
            pltpu.VMEM((rows * heads, context), F32),
            pltpu.VMEM((rows * heads, HD), F32),
            pltpu.VMEM((rows * heads, context), BF),
            pltpu.VMEM((rows * heads, HD), F32),
            pltpu.VMEM((rows, heads, HD), F32),
            pltpu.SemaphoreType.DMA((5,)),
            pltpu.SemaphoreType.DMA((chunks,)),
            pltpu.SemaphoreType.DMA((chunks,)),
        ],
        compiler_params=pltpu.CompilerParams(vmem_limit_bytes=48 << 20),
        name="attend",
    )(*map(in_hbm, (slots, lens, queries, new_keys, new_values, key_cache, value_cache)))


def project_kernel(x_ref, w00, w01, w10, w11, out_ref):
    parts, rows = out_ref.shape[0], out_ref.shape[1]
    g = lax.axis_index("g")

    def stack(side):
        return jnp.concatenate([x_ref[p, side].astype(F32) for p in range(parts)], axis=0).astype(BF)

    mine, theirs = stack(g), stack(1 - g)
    half = w00.shape[0]
    total = dot(mine[:, :half], w00[...], ((1,), (0,)))
    total += dot(mine[:, half:], w01[...], ((1,), (0,)))
    total += dot(theirs[:, :half], w10[...], ((1,), (0,)))
    total += dot(theirs[:, half:], w11[...], ((1,), (0,)))
    out_ref[...] = total.reshape(parts, rows, total.shape[1]).astype(BF)


def project(x, weights):
    parts, _, rows, _ = x.shape
    vmem = pl.BlockSpec(memory_space=pltpu.VMEM)
    return pl.pallas_call(
        project_kernel,
        out_shape=jax.ShapeDtypeStruct((parts, rows, weights[0].shape[1]), BF),
        in_specs=[vmem] * 5,
        out_specs=vmem,
        compiler_params=pltpu.CompilerParams(vmem_limit_bytes=32 << 20),
        name="project",
    )(x, *weights)


def join_kernel(parts_ref, residual_ref, out_ref, copies_ref):
    total = residual_ref[...].astype(F32)
    acc = parts_ref[0].astype(F32)
    for p in range(1, parts_ref.shape[0]):
        acc += parts_ref[p].astype(F32)
    total = (total + acc).astype(BF)
    out_ref[...] = total
    for c in range(copies_ref.shape[0]):
        copies_ref[c] = total


def join(parts, residual, copies):
    vmem = pl.BlockSpec(memory_space=pltpu.VMEM)
    return pl.pallas_call(
        join_kernel,
        out_shape=(
            jax.ShapeDtypeStruct(residual.shape, BF),
            jax.ShapeDtypeStruct((copies, *residual.shape), BF),
        ),
        in_specs=[vmem, vmem],
        out_specs=(vmem, vmem),
        name="join",
    )(parts, residual)


TAIL = 16


def expand_kernel(first_ref, x_ref, wg_hbm, wu_hbm, *rest):
    u_hbm, wg, wu, held, squares, staged, wsem, usem = rest[-8:]
    dests, height = staged.shape[0], staged.shape[1]
    per_dest = held.shape[0] // dests
    end = height - TAIL
    parts, rows, depth = x_ref.shape
    loads = [
        pltpu.make_async_copy(wg_hbm, wg, wsem.at[0]),
        pltpu.make_async_copy(wu_hbm, wu, wsem.at[1]),
    ]
    for load in loads:
        load.start()

    pair = 2 * rows
    for p in range(parts // 2):
        dest, half = p // 2, p % 2
        first = 8 * (dest // 2) + dest % 2 + 4 * half
        x = jnp.concatenate([x_ref[first].astype(F32), x_ref[first + 2].astype(F32)], axis=0)
        part = slice(p * pair, (p + 1) * pair)
        held[part, :] = x.astype(BF)
        folded = x[:, :HD] * x[:, :HD]
        for t in range(1, depth // HD):
            v = x[:, t * HD : (t + 1) * HD]
            folded += v * v
        squares[part, :] = folded
    ones = jnp.ones((TAIL, HD), BF)
    for d in range(dests):
        v = squares[d * per_dest : (d + 1) * per_dest, :]
        upper = v.astype(BF)
        lower = (v - upper.astype(F32)).astype(BF)
        total = dot(ones, upper, ((1,), (1,))) + dot(ones, lower, ((1,), (1,)))
        top = total.astype(BF).astype(F32)
        line = lax.broadcasted_iota(jnp.int32, total.shape, 0)
        both = jnp.where(line == 0, top, jnp.where(line == 1, total - top, 0.0))
        staged[d, end:, :] = jnp.zeros((TAIL, HD), BF)
        staged[d, end:, 0:per_dest] = both.astype(BF)

    to = pl.ds(first_ref[0] * dests, dests)
    cuts = ((0, end // 2), (end // 2, end // 2 + TAIL))
    outs = []
    for k, w in enumerate((wg, wu)):
        loads[k].wait()
        for lane in range(0, w.shape[1], 2 * HD):
            width = min(2 * HD, w.shape[1] - lane)
            y = dot(held[...], w[:, lane : lane + width], ((1,), (0,))).astype(BF)
            for c in range(width // HD):
                row = k * (end // 2) + (lane // HD + c) * per_dest
                for d in range(dests):
                    staged[d, row : row + per_dest, :] = y[d * per_dest : (d + 1) * per_dest, c * HD : (c + 1) * HD]
        cut = pl.ds(*cuts[k])
        outs.append(pltpu.make_async_copy(staged.at[:, cut], u_hbm.at[to, cut], usem.at[k]))
        outs[k].start()
    for out in outs:
        out.wait()


def expand(first, x, wg, wu, so_far):
    parts, rows, depth = x.shape
    dests = 4
    per_dest = parts * rows // dests
    height = wg.shape[1] // HD * 2 * per_dest + TAIL
    hbm = pl.BlockSpec(memory_space=pltpu.HBM)
    specs = [pl.BlockSpec(memory_space=pltpu.SMEM), pl.BlockSpec(memory_space=pltpu.VMEM), hbm, hbm]
    args = [first, x, in_hbm(wg), in_hbm(wu)]
    aliases = {}
    if so_far is not None:
        specs.append(hbm)
        args.append(so_far)
        aliases = {4: 0}
    return pl.pallas_call(
        expand_kernel,
        out_shape=jax.ShapeDtypeStruct((8, height, HD), BF),
        in_specs=specs,
        out_specs=hbm,
        scratch_shapes=[
            pltpu.VMEM(wg.shape, BF),
            pltpu.VMEM(wu.shape, BF),
            pltpu.VMEM((parts * rows, depth), BF),
            pltpu.VMEM((parts * rows, HD), F32),
            pltpu.VMEM((dests, height, HD), BF),
            pltpu.SemaphoreType.DMA((2,)),
            pltpu.SemaphoreType.DMA((2,)),
        ],
        input_output_aliases=aliases,
        compiler_params=pltpu.CompilerParams(vmem_limit_bytes=32 << 20),
        name="expand",
    )(*args)


def activate_kernel(u_ref, out_ref):
    per_dest = out_ref.shape[0]
    end = u_ref.shape[1] - TAIL
    s = u_ref[0, end:, :].astype(F32)
    for p in range(1, u_ref.shape[0]):
        s += u_ref[p, end:, :].astype(F32)
    square = jnp.broadcast_to(s[0:1, :] + s[1:2, :], (HD, HD)).T
    scale = lax.rsqrt(square[:per_dest, :] / D + EPS)
    def added(start):
        total = u_ref[0, start : start + per_dest].astype(F32)
        for p in range(1, u_ref.shape[0]):
            total += u_ref[p, start : start + per_dest].astype(F32)
        return total * scale

    for c in range(end // (2 * per_dest)):
        gate = added(c * per_dest)
        up = added(end // 2 + c * per_dest)
        out_ref[:, c * HD : (c + 1) * HD] = (gate / (1.0 + jnp.exp(-gate)) * up).astype(BF)


def activate(u, per_dest):
    columns = (u.shape[1] - TAIL) // (2 * per_dest) * HD
    vmem = pl.BlockSpec(memory_space=pltpu.VMEM)
    return pl.pallas_call(
        activate_kernel,
        out_shape=jax.ShapeDtypeStruct((per_dest, columns), BF),
        in_specs=[vmem],
        out_specs=vmem,
        compiler_params=pltpu.CompilerParams(vmem_limit_bytes=32 << 20),
        name="activate",
    )(u)


def swapped(x, axis):
    return lax.ppermute(x, axis, [(0, 1), (1, 0)])


def exchange(x, axes):
    return lax.all_to_all(x, axes, 0, 0, tiled=True)


def scalar(*values):
    return jnp.stack([jnp.asarray(v, jnp.int32) for v in values])


def body(queries, new_keys, new_values, key_cache, value_cache, context_len, cache_slot,
         residual_in, out_weight, gate_weight, up_weight):
    rows = queries.shape[0]
    g = lax.axis_index("g")

    attended = attend(8, cache_slot, context_len, queries, new_keys, new_values, key_cache, value_cache)
    attended, out_weight = lax.optimization_barrier((attended, out_weight))
    w01 = swapped(out_weight, "z0")
    heads, w01, late = lax.optimization_barrier((exchange(attended, MC), w01, out_weight))
    w10 = swapped(late, "g")
    w11 = swapped(w01, "g")
    heads = heads.reshape(2, 4, *heads.shape[1:]).transpose(1, 2, 0, 3, 4)
    heads = heads.reshape(8, *heads.shape[2:])
    partial = project(exchange(heads, KAPPA), (out_weight, w01, w10, w11))
    residual_out, copies = join(exchange(partial, KAPPA), residual_in, 16)
    mine = exchange(copies, ("zh", "z1", "z0", "yl"))
    theirs = swapped(mine, "g")
    u = expand(scalar(g), mine, gate_weight, up_weight, None)
    u = expand(scalar(1 - g), theirs, gate_weight, up_weight, u)
    activation = activate(exchange(u, ("yh", "xl", "xh")), 4 * rows)
    return (residual_out, activation)


def solution(mesh):
    fine = Mesh(mesh.devices.reshape((2,) * 8), FINE)
    r = ("g",) + YLZ
    in_specs = (P(r, MC), P(r, MC), P(r, MC), P(r, None, MC), P(r, None, MC), P(r), P(r), P(r, MC),
                P(r, MC), P(MC, r), P(MC, r))
    out_specs = (P(r, MC), P(MC, r))
    return jax.shard_map(body, mesh=fine, in_specs=in_specs, out_specs=out_specs, check_vma=False)
```
